256 devices in a mesh: lev: 8 (over z_hi, y), tile: 32 (over z_lo, x, core).
Axes of the slice: x: 4, y: 4, z: 8 (z_hi: 2, z_lo: 4; z = z_hi * 4 + z_lo), core: 2. Of those that a mesh axis runs over, the one named last changes fastest.
Arguments:
- prognostic: float32 [4, 128, 262144], P(None, 'lev', 'tile'), may hold values from -6 to 6
- neighbours: int32 [4, 262144], P(None, 'tile'), may hold values from 0 to 8447, as said below
- metric: float32 [2, 4, 262144], P(None, None, 'tile'), may hold values from -0.9 to 0.9
- inverses: float32 [32, 128, 128], P('tile')
Outputs:
- advanced: float32 [4, 128, 262144], P(None, 'lev', 'tile')
The draws below stay inside these ranges and needn't reach their ends.
Inputs may be any that keep to these rules, and one draw needn't show every extreme that they name: `neighbours`: entry [k, c] indexes the cells of c's tile extended by 128 cells on each side: 0 to 127 are the last 128 cells of the previous tile, then the tile's own 8192 cells in order, then the first 128 cells of the next tile, the tiles forming a closed cycle; each entry lies within 128 of 128 + (c mod 8192).
All inputs are finite; a program needn't handle non-finite values.
Results may differ from the reference program's by a relative error of at most 0.0001.
Values sent between devices are 32-bit elements; how exact they have to be, the bound alone decides.
A program may use at most 64 MiB of HBM per device.

```python
import math
import jax
import jax.numpy as jnp
from jax import lax

NLEV = 128
CELLS_DEV = 8192
NB = 4
HALO = 128
SUBSTEPS = 3
CELLS = 262144
REGIONS = 32


def draw_neighbours(key, part):
    offsets = jax.random.randint(key, (NB, CELLS), -HALO, HALO + 1)
    position = jnp.arange(CELLS, dtype=jnp.int32) % CELLS_DEV
    local_index = HALO + position[None, :] + offsets
    first_row = jnp.arange(NB, dtype=jnp.int32)[:, None] == 0
    local_index = jnp.where(first_row & (position[None, :] == 0), 0, local_index)
    local_index = jnp.where(first_row & (position[None, :] == CELLS_DEV - 1), CELLS_DEV + 2 * HALO - 1, local_index)
    return local_index.astype(jnp.int32)


def draw_inverses(key, part):
    array_shape = (REGIONS, NLEV, NLEV)
    random_part = jnp.clip(jax.random.normal(key, array_shape, jnp.float32), -6.0, 6.0)
    row_index = lax.broadcasted_iota(jnp.int32, array_shape, 1)
    col_index = lax.broadcasted_iota(jnp.int32, array_shape, 2)
    diagonal = jnp.where(row_index == col_index, 1.0, 0.0).astype(jnp.float32)
    return diagonal + 0.25 / math.sqrt(NLEV) * random_part


def steps_of(own_key, shape, cuts, smallest, high):
    factor_of = 1.0
    for dim, shards_of in cuts:
        steps = jax.random.uniform(jax.random.fold_in(jax.random.fold_in(own_key, 6), dim), (shards_of,), jnp.float32, smallest / len(cuts), high / len(cuts))
        factor_of = factor_of * jnp.repeat(jnp.exp(steps), shape[dim] // shards_of).reshape((-1,) + (1,) * (len(shape) - 1 - dim))
    return factor_of


def noise(own_key, dims, scale, reach, shards=(), held_as=jnp.bfloat16):
    array = scale * jax.random.normal(own_key, dims, jnp.float32)
    if shards:
        array = array * steps_of(own_key, dims, shards, -0.22, 0.18)
    return jnp.clip(array, -reach, reach).astype(held_as)


def setup_inputs(seed: int = 0) -> dict:
    arg_keys = jax.random.split(jax.random.key(seed), 5)
    prognostic = noise(arg_keys[0], (4, NLEV, CELLS), 1.0, 6.0, ((1, 8), (2, 32)), jnp.float32)
    neighbours = draw_neighbours(jax.random.fold_in(arg_keys[4], 71), 0)
    metric = noise(arg_keys[2], (2, NB, CELLS), 0.15, 0.9, ((2, 32),), jnp.float32)
    inverses = draw_inverses(jax.random.fold_in(arg_keys[4], 71), 0)
    return dict(prognostic=prognostic, neighbours=neighbours, metric=metric, inverses=inverses)


acoustic = 0.4


def level_slope(padded):
    return 0.5 * (padded[2:] - padded[:-2])


def pad_levels(field):
    return jnp.pad(field, ((1, 1), (0, 0)))


def horizontal_step(moving, neighbours, metric):
    cell_count = moving.shape[2]
    position = jnp.arange(cell_count, dtype=jnp.int32)
    anchor = (position // CELLS_DEV) * CELLS_DEV - HALO
    gradient_east = jnp.zeros(moving.shape[1:], moving.dtype)
    gradient_north = jnp.zeros(moving.shape[1:], moving.dtype)
    diverge = jnp.zeros(moving.shape[1:], moving.dtype)
    for direction in range(NB):
        global_index = ((anchor + neighbours[direction]) % cell_count).astype(jnp.int32)
        nearby = jnp.take(moving, global_index, axis=2)
        change = nearby - moving
        weight_east = metric[0, direction]
        weight_north = metric[1, direction]
        gradient_east = gradient_east + weight_east * change[2]
        gradient_north = gradient_north + weight_north * change[2]
        diverge = diverge + (weight_east * change[0] + weight_north * change[1])
    return moving[0] - gradient_east, moving[1] - gradient_north, moving[2] - diverge


def reference(prognostic, neighbours, metric, inverses):
    fields = prognostic
    for substep in range(SUBSTEPS):
        east, north, pressure = horizontal_step(fields[:3], neighbours, metric)
        right_side = fields[3] - acoustic * level_slope(pad_levels(pressure))
        tiled = right_side.reshape(NLEV, REGIONS, CELLS_DEV)
        solved = jnp.einsum("tij,jtc->itc", inverses, tiled, precision=lax.Precision.HIGHEST)
        vertical = solved.reshape(NLEV, CELLS)
        pressure = pressure - acoustic * level_slope(pad_levels(vertical))
        fields = jnp.stack([east, north, pressure, vertical])
    return fields
```

```python
import functools

import jax
import jax.numpy as jnp
from jax import lax
from jax.experimental import pallas as pl
from jax.experimental.pallas import tpu as pltpu
from jax.sharding import PartitionSpec as P

SUBSTEPS = 3
NB = 4
HALO = 128
NY = 4
BLOCK = 256
LAG = 4
F32, BF16 = jnp.float32, jnp.bfloat16
C = 0.4 * 0.5


def split(x):
    high = x.astype(BF16)
    return high, (x - high.astype(F32)).astype(BF16)


def dot(a, b):
    return jnp.dot(a, b, preferred_element_type=F32)


def kernel(prog, nbrs, metr, inv, out, X, PP, RS, RR, PB, PQ, M, NBV, MTV, IH, IL,
           lsem, yin_s, yin_r, yin_l, out_s, out_r, out_l, z_s, z_r, b_s, b_r, h_s, h_r):
    lev, tile = lax.axis_index("lev"), lax.axis_index("tile")
    zh, y = lev // NY, lev % NY
    tiles = lax.axis_size("tile")
    half = X.shape[2]
    rows16 = half // NY
    slab = PP.shape[2]
    blocks = slab // BLOCK
    total = SUBSTEPS * blocks

    def at(yy, tt):
        return {"lev": zh * NY + yy, "tile": tt}

    peers = [at((y + d) % NY, tile) for d in range(NY)]
    partner = {"lev": (1 - zh) * NY + y, "tile": tile}
    right = at((y + 1) % NY, (tile + jnp.where(y == NY - 1, 1, 0)) % tiles)
    left = at((y + NY - 1) % NY, (tile + jnp.where(y == 0, tiles - 1, 0)) % tiles)

    def remote(src, dst, ssem, rsem, dev):
        return pltpu.make_async_remote_copy(src, dst, ssem, rsem, device_id=dev, device_id_type=pl.DeviceIdType.MESH)

    def order(i):
        return jnp.where(i % 2 == 0, i // 2, blocks - 1 - i // 2)

    def cells(c):
        return pl.ds(pl.multiple_of(HALO + c * BLOCK, 128), BLOCK)

    def lanes(c):
        return pl.ds(pl.multiple_of(c * BLOCK, 128), BLOCK)

    def y_in(c, d):
        yy = (y + d) % NY
        src = prog.at[:, :, pl.ds(pl.multiple_of(yy * slab + c * BLOCK, 128), BLOCK)]
        dst = X.at[0, :, pl.ds(pl.multiple_of(y * rows16, 8), rows16), cells(c)]
        if d == 0:
            return pltpu.make_async_copy(src, dst, yin_l.at[c])
        return remote(src, dst, yin_s.at[c, d - 1], yin_r.at[c, d - 1], peers[d])

    def y_in_start(c):
        for d in range(NY):
            y_in(c, d).start()

    def y_in_wait(c):
        y_in(c, 0).wait()
        for d in range(1, NY):
            y_in(c, d).wait_recv()

    def y_out(f, c, d):
        yy = (y + d) % NY
        src = X.at[SUBSTEPS, pl.ds(2 * f, 2), pl.ds(pl.multiple_of(yy * rows16, 8), rows16), cells(c)]
        dst = out.at[pl.ds(2 * f, 2), :, pl.ds(pl.multiple_of(y * slab + c * BLOCK, 128), BLOCK)]
        if d == 0:
            return pltpu.make_async_copy(src, dst, out_l.at[f, c])
        return remote(src, dst, out_s.at[f, c, d - 1], out_r.at[f, c, d - 1], peers[d])

    def z_copies(s, c):
        return (
            remote(RS.at[s, :, lanes(c)], RR.at[s, :, lanes(c)], z_s.at[s, c], z_r.at[s, c], partner),
            remote(PB.at[s, c], PQ.at[s, c], b_s.at[s, c], b_r.at[s, c], partner),
        )

    def halo(s, side):
        if side == 0:
            src, dst, dev = pl.ds(HALO, HALO), pl.ds(HALO + slab, HALO), left
        else:
            src, dst, dev = pl.ds(slab, HALO), pl.ds(0, HALO), right
        return remote(X.at[s, pl.ds(0, 3), :, src], X.at[s, pl.ds(0, 3), :, dst], h_s.at[s, side], h_r.at[s, side], dev)

    barrier = pltpu.get_barrier_semaphore()
    others = peers[1:] + [partner, left, right]
    for dev in others:
        pl.semaphore_signal(barrier, 1, device_id=dev, device_id_type=pl.DeviceIdType.MESH)
    local = (
        pltpu.make_async_copy(nbrs.at[:, pl.ds(pl.multiple_of(y * slab, 128), slab)], NBV, lsem.at[0]),
        pltpu.make_async_copy(metr.at[:, :, pl.ds(pl.multiple_of(y * slab, 128), slab)], MTV, lsem.at[1]),
    )
    for copy in local:
        copy.start()
    pl.semaphore_wait(barrier, len(others))
    for i in range(3):
        y_in_start(order(i))
    for copy in local:
        copy.wait()

    full = inv[0]
    swapped = jnp.where(zh == 0, full, pltpu.roll(full, half, 1))
    mine = jnp.concatenate([
        jnp.where(zh == 0, swapped[:half], swapped[half:]),
        jnp.where(zh == 0, swapped[half:half + 8], swapped[half - 8:half]),
    ])
    IH[...], IL[...] = split(mine)

    level = lax.broadcasted_iota(jnp.int32, (half, BLOCK), 0)
    first, last = level == 0, level == half - 1

    def build(c):
        def rows(j, carry):
            r0 = pl.multiple_of(j * 64, 64)
            slot = lax.broadcasted_iota(jnp.int32, (64, BLOCK), 0) + r0
            cell = lax.broadcasted_iota(jnp.int32, (64, BLOCK), 1)
            here = slot == cell + HALO
            m0 = jnp.zeros((64, BLOCK), F32)
            m1 = jnp.zeros((64, BLOCK), F32)
            for k in range(NB):
                w0, w1 = MTV[0, pl.ds(k, 1), lanes(c)], MTV[1, pl.ds(k, 1), lanes(c)]
                hit = slot == NBV[pl.ds(k, 1), lanes(c)] - (y * slab + c * BLOCK)
                m0 = m0 + (jnp.where(hit, w0, 0.0) - jnp.where(here, w0, 0.0))
                m1 = m1 + (jnp.where(hit, w1, 0.0) - jnp.where(here, w1, 0.0))
            M[c, 0, pl.ds(r0, 64), :], M[c, 1, pl.ds(r0, 64), :] = split(m0)
            M[c, 2, pl.ds(r0, 64), :], M[c, 3, pl.ds(r0, 64), :] = split(m1)
            return carry

        lax.fori_loop(0, (BLOCK + 2 * HALO) // 64, rows, 0)

    def horizontal(s, c):
        window = pl.ds(pl.multiple_of(c * BLOCK, 128), BLOCK + 2 * HALO)
        uh, ul = split(X[s, 0, :, window])
        vh, vl = split(X[s, 1, :, window])
        ph, pl_ = split(X[s, 2, :, window])
        a0 = dot(jnp.concatenate([ph, uh, pl_, ul]), M[c, 0])
        b0 = dot(jnp.concatenate([ph, uh]), M[c, 1])
        a1 = dot(jnp.concatenate([ph, vh, pl_, vl]), M[c, 2])
        b1 = dot(jnp.concatenate([ph, vh]), M[c, 3])
        g0 = a0[: 2 * half] + a0[2 * half :] + b0
        g1 = a1[: 2 * half] + a1[2 * half :] + b1
        X[s + 1, 0, :, cells(c)] = X[s, 0, :, cells(c)] - g0[:half]
        X[s + 1, 1, :, cells(c)] = X[s, 1, :, cells(c)] - g1[:half]
        p = X[s, 2, :, cells(c)] - (g0[half:] + g1[half:])
        PP[s, :, lanes(c)] = p
        up = jnp.where(last, 0.0, pltpu.roll(p, half - 1, 0))
        down = jnp.where(first, 0.0, pltpu.roll(p, 1, 0))
        RS[s, :, lanes(c)] = X[s, 3, :, cells(c)] - C * (up - down)
        PB[s, c] = jnp.where(zh == 0, p[half - 1 :], p[:1])

    def vertical(s, c):
        top = jnp.where(zh == 0, 1.0, 0.0)
        own_b, other_b = PB[s, c], PQ[s, c]
        fix_own = jnp.where(last, -C * top, 0.0) + jnp.where(first, C * (1.0 - top), 0.0)
        fix_other = jnp.where(first, C * top, 0.0) + jnp.where(last, -C * (1.0 - top), 0.0)
        own = RS[s, :, lanes(c)] + fix_own * other_b
        other = RR[s, :, lanes(c)] + fix_other * own_b
        rh, rl = split(jnp.concatenate([own, other]))
        ih, il = IH[...], IL[...]
        w = dot(ih, rh) + (dot(ih, rl) + dot(il, rh))
        edge = jnp.where(zh == 0, w[half : half + 1], w[half + 7 : half + 8])
        w = w[:half]
        up = jnp.where(last, edge * top, pltpu.roll(w, half - 1, 0))
        down = jnp.where(first, edge * (1.0 - top), pltpu.roll(w, 1, 0))
        X[s + 1, 2, :, cells(c)] = PP[s, :, lanes(c)] - C * (up - down)
        X[s + 1, 3, :, cells(c)] = w

    def finish(t):
        s, c = t // blocks, order(t % blocks)
        for copy in z_copies(s, c):
            copy.wait_recv()
        vertical(s, c)

        @pl.when((s < SUBSTEPS - 1) & (c == 0))
        def _():
            halo(s + 1, 0).start()

        @pl.when((s < SUBSTEPS - 1) & (c == blocks - 1))
        def _():
            halo(s + 1, 1).start()

        @pl.when(s == SUBSTEPS - 1)
        def _():
            for d in range(NY):
                y_out(1, c, d).start()

    def begin(t):
        s, i = t // blocks, t % blocks
        c = order(i)

        @pl.when(s == 0)
        def _():
            @pl.when(i + 3 < blocks)
            def _():
                y_in_start(order(i + 3))

            build(c)

            @pl.when(i == 0)
            def _():
                y_in_wait(0)
                halo(0, 0).start()
                y_in_wait(blocks - 1)
                halo(0, 1).start()

            @pl.when(i + 2 < blocks)
            def _():
                y_in_wait(order(i + 2))

        @pl.when(i == 0)
        def _():
            halo(s, 1).wait_recv()

        @pl.when(i == 1)
        def _():
            halo(s, 0).wait_recv()

        horizontal(s, c)
        for copy in z_copies(s, c):
            copy.start()

        @pl.when(s == SUBSTEPS - 1)
        def _():
            for d in range(NY):
                y_out(0, c, d).start()

    def step(t, carry):
        @pl.when(t >= LAG)
        def _():
            finish(t - LAG)

        @pl.when(t < total)
        def _():
            begin(t)

        return carry

    lax.fori_loop(0, total + LAG, step, 0)

    def drain(c, carry):
        for d in range(1, NY):
            y_in(c, d).wait_send()
        for f in range(2):
            y_out(f, c, 0).wait()
            for d in range(1, NY):
                y_out(f, c, d).wait()
        for s in range(SUBSTEPS):
            for copy in z_copies(s, c):
                copy.wait_send()
        return carry

    lax.fori_loop(0, blocks, drain, 0)
    for s in range(SUBSTEPS):
        for side in range(2):
            halo(s, side).wait_send()


def per_device(prognostic, neighbours, metric, inverses):
    fields, rows16, cell_count = prognostic.shape
    half, slab = rows16 * NY, cell_count // NY
    blocks = slab // BLOCK
    dma = pltpu.SemaphoreType.DMA
    anywhere = pl.BlockSpec(memory_space=pl.ANY)
    return pl.pallas_call(
        kernel,
        name="acoustic",
        out_shape=jax.ShapeDtypeStruct(prognostic.shape, F32),
        in_specs=[anywhere, anywhere, anywhere, pl.BlockSpec(memory_space=pltpu.VMEM)],
        out_specs=anywhere,
        scratch_shapes=[
            pltpu.VMEM((SUBSTEPS + 1, fields, half, slab + 2 * HALO), F32),
            pltpu.VMEM((SUBSTEPS, half, slab), F32),
            pltpu.VMEM((SUBSTEPS, half, slab), F32),
            pltpu.VMEM((SUBSTEPS, half, slab), F32),
            pltpu.VMEM((SUBSTEPS, blocks, 1, BLOCK), F32),
            pltpu.VMEM((SUBSTEPS, blocks, 1, BLOCK), F32),
            pltpu.VMEM((blocks, 4, BLOCK + 2 * HALO, BLOCK), BF16),
            pltpu.VMEM((NB, slab), jnp.int32),
            pltpu.VMEM((2, NB, slab), F32),
            pltpu.VMEM((half + 8, 2 * half), BF16),
            pltpu.VMEM((half + 8, 2 * half), BF16),
            dma((2,)),
            dma((blocks, NY - 1)),
            dma((blocks, NY - 1)),
            dma((blocks,)),
            dma((2, blocks, NY - 1)),
            dma((2, blocks, NY - 1)),
            dma((2, blocks)),
            dma((SUBSTEPS, blocks)),
            dma((SUBSTEPS, blocks)),
            dma((SUBSTEPS, blocks)),
            dma((SUBSTEPS, blocks)),
            dma((SUBSTEPS, 2)),
            dma((SUBSTEPS, 2)),
        ],
        compiler_params=pltpu.CompilerParams(
            collective_id=0, has_side_effects=True, vmem_limit_bytes=48 << 20
        ),
    )(prognostic, neighbours, metric, inverses)


def solution(mesh):
    in_specs = (
        P(None, "lev", "tile"),
        P(None, "tile"),
        P(None, None, "tile"),
        P("tile", None, None),
    )
    return jax.shard_map(
        per_device, mesh=mesh, in_specs=in_specs, out_specs=P(None, "lev", "tile"), check_vma=False
    )
```

```python
import functools

import jax
import jax.numpy as jnp
from jax import lax
from jax.experimental import pallas as pl
from jax.experimental.pallas import tpu as pltpu
from jax.sharding import PartitionSpec as P

SUBSTEPS = 3
NB = 4
HALO = 128
NY = 4
BLOCK = 256
LAG = 4
AHEAD = 4
F32, BF16 = jnp.float32, jnp.bfloat16
C = 0.4 * 0.5


def split(x):
    high = x.astype(BF16)
    return high, (x - high.astype(F32)).astype(BF16)


def dot(a, b):
    return jnp.dot(a, b, preferred_element_type=F32)


def kernel(prog, nbrs, metr, inv, out, X, PP, RS, RR, PB, PQ, M, IV, NBV, MTV, IH, IL,
           lsem, yin_s, yin_r, yin_l, out_s, out_r, out_l, z_s, z_r, b_s, b_r, h_s, h_r, e_s, e_r, e_l):
    lev, tile = lax.axis_index("lev"), lax.axis_index("tile")
    zh, y = lev // NY, lev % NY
    tiles = lax.axis_size("tile")
    half = X.shape[2]
    rows16 = half // NY
    slab = PP.shape[2]
    blocks = slab // BLOCK
    total = SUBSTEPS * blocks
    cell_count = prog.shape[2]

    def at(yy, tt):
        return {"lev": zh * NY + yy, "tile": tt}

    peers = [at((y + d) % NY, tile) for d in range(NY)]
    partner = {"lev": (1 - zh) * NY + y, "tile": tile}
    right = at((y + 1) % NY, (tile + jnp.where(y == NY - 1, 1, 0)) % tiles)
    left = at((y + NY - 1) % NY, (tile + jnp.where(y == 0, tiles - 1, 0)) % tiles)

    def remote(src, dst, ssem, rsem, dev):
        return pltpu.make_async_remote_copy(src, dst, ssem, rsem, device_id=dev, device_id_type=pl.DeviceIdType.MESH)

    def order(s, i):
        one = jnp.where(i < blocks - 2, i + 1, jnp.where(i == blocks - 2, 0, blocks - 1))
        two = jnp.where(i < blocks - 4, i + 2, jnp.where(i == blocks - 4, 1, jnp.where(i == blocks - 3, blocks - 2, one)))
        return jnp.where(s == 0, i, jnp.where(s == 1, one, two))

    def cells(c):
        return pl.ds(pl.multiple_of(HALO + c * BLOCK, 128), BLOCK)

    def lanes(c):
        return pl.ds(pl.multiple_of(c * BLOCK, 128), BLOCK)

    def y_in(c, d):
        yy = (y + d) % NY
        src = prog.at[:, :, pl.ds(pl.multiple_of(yy * slab + c * BLOCK, 128), BLOCK)]
        dst = X.at[0, :, pl.ds(pl.multiple_of(y * rows16, 8), rows16), cells(c)]
        if d == 0:
            return pltpu.make_async_copy(src, dst, yin_l.at[c])
        return remote(src, dst, yin_s.at[c, d - 1], yin_r.at[c, d - 1], peers[d])

    def edge(side, d, local=False):
        yy = (y + d) % NY
        own = pl.multiple_of(y * rows16, 8)
        if side == 0:
            first, put = (yy * slab + cell_count - HALO) % cell_count, 0
            dev = at(yy, (tile + jnp.where(yy == 0, 1, 0)) % tiles)
        else:
            first, put = ((yy + 1) * slab) % cell_count, HALO + slab
            dev = at(yy, (tile + jnp.where(yy == NY - 1, tiles - 1, 0)) % tiles)
        src = prog.at[pl.ds(0, 3), :, pl.ds(pl.multiple_of(first, 128), HALO)]
        dst = X.at[0, pl.ds(0, 3), pl.ds(own, rows16), pl.ds(put, HALO)]
        if local:
            return pltpu.make_async_copy(src, dst, e_l.at[side])
        return remote(src, dst, e_s.at[side, d], e_r.at[side, d], dev)

    outer = (0, NY - 1)

    def edge_start(side):
        for d in range(1, NY):
            edge(side, d).start()
        pl.when(y == outer[side])(lambda: edge(side, 0).start())
        pl.when(y != outer[side])(lambda: edge(side, 0, True).start())

    def edge_wait(side):
        for d in range(1, NY):
            edge(side, d).wait_recv()
        pl.when(y == outer[side])(lambda: edge(side, 0).wait_recv())
        pl.when(y != outer[side])(lambda: edge(side, 0, True).wait())

    def edge_drain(side):
        for d in range(1, NY):
            edge(side, d).wait_send()
        pl.when(y == outer[side])(lambda: edge(side, 0).wait_send())

    def y_in_start(c):
        for d in range(NY):
            y_in(c, d).start()

    def y_in_wait(c):
        y_in(c, 0).wait()
        for d in range(1, NY):
            y_in(c, d).wait_recv()

    def y_out(f, c, d):
        yy = (y + d) % NY
        src = X.at[SUBSTEPS, pl.ds(2 * f, 2), pl.ds(pl.multiple_of(yy * rows16, 8), rows16), cells(c)]
        dst = out.at[pl.ds(2 * f, 2), :, pl.ds(pl.multiple_of(y * slab + c * BLOCK, 128), BLOCK)]
        if d == 0:
            return pltpu.make_async_copy(src, dst, out_l.at[f, c])
        return remote(src, dst, out_s.at[f, c, d - 1], out_r.at[f, c, d - 1], peers[d])

    def z_copies(s, c):
        return (
            remote(RS.at[s, :, lanes(c)], RR.at[s, :, lanes(c)], z_s.at[s, c], z_r.at[s, c], partner),
            remote(PB.at[s, c], PQ.at[s, c], b_s.at[s, c], b_r.at[s, c], partner),
        )

    def halo(s, side):
        if side == 0:
            src, dst, dev = pl.ds(HALO, HALO), pl.ds(HALO + slab, HALO), left
        else:
            src, dst, dev = pl.ds(slab, HALO), pl.ds(0, HALO), right
        return remote(X.at[s, pl.ds(0, 3), :, src], X.at[s, pl.ds(0, 3), :, dst], h_s.at[s, side], h_r.at[s, side], dev)

    barrier = pltpu.get_barrier_semaphore()
    others = peers[1:] + [partner, left, right]
    for dev in others:
        pl.semaphore_signal(barrier, 1, device_id=dev, device_id_type=pl.DeviceIdType.MESH)
    for side in range(2):
        @pl.when(y == outer[side])
        def _():
            for yy in range(NY):
                dev = at(yy, (tile + (1 if side else tiles - 1)) % tiles)
                pl.semaphore_signal(barrier, 1, device_id=dev, device_id_type=pl.DeviceIdType.MESH)

    local = (
        pltpu.make_async_copy(nbrs.at[:, pl.ds(pl.multiple_of(y * slab, 128), slab)], NBV, lsem.at[0]),
        pltpu.make_async_copy(metr.at[:, :, pl.ds(pl.multiple_of(y * slab, 128), slab)], MTV, lsem.at[1]),
    )
    local = local + (pltpu.make_async_copy(inv.at[0], IV, lsem.at[2]),)
    for copy in local:
        copy.start()
    pl.semaphore_wait(barrier, len(others) + 2)
    edge_start(0)
    for c in range(AHEAD):
        y_in_start(c)
    edge_start(1)
    for copy in local:
        copy.wait()

    full = IV[...]
    swapped = jnp.where(zh == 0, full, pltpu.roll(full, half, 1))
    mine = jnp.concatenate([
        jnp.where(zh == 0, swapped[:half], swapped[half:]),
        jnp.where(zh == 0, swapped[half:half + 8], swapped[half - 8:half]),
    ])
    IH[...], IL[...] = split(mine)

    level = lax.broadcasted_iota(jnp.int32, (half, BLOCK), 0)
    first, last = level == 0, level == half - 1

    def build(c):
        def rows(j, carry):
            r0 = pl.multiple_of(j * 64, 64)
            slot = lax.broadcasted_iota(jnp.int32, (64, BLOCK), 0) + r0
            cell = lax.broadcasted_iota(jnp.int32, (64, BLOCK), 1)
            here = slot == cell + HALO
            m0 = jnp.zeros((64, BLOCK), F32)
            m1 = jnp.zeros((64, BLOCK), F32)
            for k in range(NB):
                w0, w1 = MTV[0, pl.ds(k, 1), lanes(c)], MTV[1, pl.ds(k, 1), lanes(c)]
                hit = slot == NBV[pl.ds(k, 1), lanes(c)] - (y * slab + c * BLOCK)
                m0 = m0 + (jnp.where(hit, w0, 0.0) - jnp.where(here, w0, 0.0))
                m1 = m1 + (jnp.where(hit, w1, 0.0) - jnp.where(here, w1, 0.0))
            M[c, 0, pl.ds(r0, 64), :], M[c, 1, pl.ds(r0, 64), :] = split(m0)
            M[c, 2, pl.ds(r0, 64), :], M[c, 3, pl.ds(r0, 64), :] = split(m1)
            return carry

        lax.fori_loop(0, (BLOCK + 2 * HALO) // 64, rows, 0)

    def horizontal(s, c):
        window = pl.ds(pl.multiple_of(c * BLOCK, 128), BLOCK + 2 * HALO)
        uh, ul = split(X[s, 0, :, window])
        vh, vl = split(X[s, 1, :, window])
        ph, pl_ = split(X[s, 2, :, window])
        a0 = dot(jnp.concatenate([ph, uh, pl_, ul]), M[c, 0])
        b0 = dot(jnp.concatenate([ph, uh]), M[c, 1])
        a1 = dot(jnp.concatenate([ph, vh, pl_, vl]), M[c, 2])
        b1 = dot(jnp.concatenate([ph, vh]), M[c, 3])
        g0 = a0[: 2 * half] + a0[2 * half :] + b0
        g1 = a1[: 2 * half] + a1[2 * half :] + b1
        X[s + 1, 0, :, cells(c)] = X[s, 0, :, cells(c)] - g0[:half]
        X[s + 1, 1, :, cells(c)] = X[s, 1, :, cells(c)] - g1[:half]
        p = X[s, 2, :, cells(c)] - (g0[half:] + g1[half:])
        PP[s, :, lanes(c)] = p
        up = jnp.where(last, 0.0, pltpu.roll(p, half - 1, 0))
        down = jnp.where(first, 0.0, pltpu.roll(p, 1, 0))
        RS[s, :, lanes(c)] = X[s, 3, :, cells(c)] - C * (up - down)
        PB[s, c] = jnp.where(zh == 0, p[half - 1 :], p[:1])

    def vertical(s, c):
        top = jnp.where(zh == 0, 1.0, 0.0)
        own_b, other_b = PB[s, c], PQ[s, c]
        fix_own = jnp.where(last, -C * top, 0.0) + jnp.where(first, C * (1.0 - top), 0.0)
        fix_other = jnp.where(first, C * top, 0.0) + jnp.where(last, -C * (1.0 - top), 0.0)
        own = RS[s, :, lanes(c)] + fix_own * other_b
        other = RR[s, :, lanes(c)] + fix_other * own_b
        rh, rl = split(jnp.concatenate([own, other]))
        ih, il = IH[...], IL[...]
        w = dot(ih, rh) + (dot(ih, rl) + dot(il, rh))
        edge = jnp.where(zh == 0, w[half : half + 1], w[half + 7 : half + 8])
        w = w[:half]
        up = jnp.where(last, edge * top, pltpu.roll(w, half - 1, 0))
        down = jnp.where(first, edge * (1.0 - top), pltpu.roll(w, 1, 0))
        X[s + 1, 2, :, cells(c)] = PP[s, :, lanes(c)] - C * (up - down)
        X[s + 1, 3, :, cells(c)] = w

    def finish(t):
        s, c = t // blocks, order(t // blocks, t % blocks)
        for copy in z_copies(s, c):
            copy.wait_recv()
        vertical(s, c)

        @pl.when((s < SUBSTEPS - 1) & (c == 0))
        def _():
            halo(s + 1, 0).start()

        @pl.when((s < SUBSTEPS - 1) & (c == blocks - 1))
        def _():
            halo(s + 1, 1).start()

        @pl.when(s == SUBSTEPS - 1)
        def _():
            for d in range(NY):
                y_out(1, c, d).start()

    def begin(t):
        s, i = t // blocks, t % blocks
        c = order(s, i)

        @pl.when(s == 0)
        def _():
            build(c)

            @pl.when(i == 0)
            def _():
                edge_wait(0)
                y_in_wait(0)

            @pl.when(i + 1 < blocks)
            def _():
                y_in_wait(i + 1)

            @pl.when(i == blocks - 1)
            def _():
                edge_wait(1)

            @pl.when(i + AHEAD < blocks)
            def _():
                y_in_start(i + AHEAD)

        @pl.when((s > 0) & (c == 0))
        def _():
            halo(s, 1).wait_recv()

        @pl.when((s > 0) & (c == blocks - 1))
        def _():
            halo(s, 0).wait_recv()

        horizontal(s, c)
        for copy in z_copies(s, c):
            copy.start()

        @pl.when(s == SUBSTEPS - 1)
        def _():
            for d in range(NY):
                y_out(0, c, d).start()

    def step(t, carry):
        @pl.when(t >= LAG)
        def _():
            finish(t - LAG)

        @pl.when(t < total)
        def _():
            begin(t)

        return carry

    lax.fori_loop(0, total + LAG, step, 0)

    def drain(c, carry):
        for d in range(1, NY):
            y_in(c, d).wait_send()
        for f in range(2):
            y_out(f, c, 0).wait()
            for d in range(1, NY):
                y_out(f, c, d).wait()
        for s in range(SUBSTEPS):
            for copy in z_copies(s, c):
                copy.wait_send()
        return carry

    lax.fori_loop(0, blocks, drain, 0)
    for side in range(2):
        edge_drain(side)
        for s in range(1, SUBSTEPS):
            halo(s, side).wait_send()


def per_device(prognostic, neighbours, metric, inverses):
    fields, rows16, cell_count = prognostic.shape
    half, slab = rows16 * NY, cell_count // NY
    blocks = slab // BLOCK
    dma = pltpu.SemaphoreType.DMA
    anywhere = pl.BlockSpec(memory_space=pltpu.HBM)
    return pl.pallas_call(
        kernel,
        name="acoustic",
        out_shape=jax.ShapeDtypeStruct(prognostic.shape, F32),
        in_specs=[anywhere, anywhere, anywhere, anywhere],
        out_specs=anywhere,
        scratch_shapes=[
            pltpu.VMEM((SUBSTEPS + 1, fields, half, slab + 2 * HALO), F32),
            pltpu.VMEM((SUBSTEPS, half, slab), F32),
            pltpu.VMEM((SUBSTEPS, half, slab), F32),
            pltpu.VMEM((SUBSTEPS, half, slab), F32),
            pltpu.VMEM((SUBSTEPS, blocks, 1, BLOCK), F32),
            pltpu.VMEM((SUBSTEPS, blocks, 1, BLOCK), F32),
            pltpu.VMEM((blocks, 4, BLOCK + 2 * HALO, BLOCK), BF16),
            pltpu.VMEM((2 * half, 2 * half), F32),
            pltpu.VMEM((NB, slab), jnp.int32),
            pltpu.VMEM((2, NB, slab), F32),
            pltpu.VMEM((half + 8, 2 * half), BF16),
            pltpu.VMEM((half + 8, 2 * half), BF16),
            dma((3,)),
            dma((blocks, NY - 1)),
            dma((blocks, NY - 1)),
            dma((blocks,)),
            dma((2, blocks, NY - 1)),
            dma((2, blocks, NY - 1)),
            dma((2, blocks)),
            dma((SUBSTEPS, blocks)),
            dma((SUBSTEPS, blocks)),
            dma((SUBSTEPS, blocks)),
            dma((SUBSTEPS, blocks)),
            dma((SUBSTEPS, 2)),
            dma((SUBSTEPS, 2)),
            dma((2, NY)),
            dma((2, NY)),
            dma((2,)),
        ],
        compiler_params=pltpu.CompilerParams(
            collective_id=0, has_side_effects=True, vmem_limit_bytes=62 << 20
        ),
    )(prognostic, neighbours, metric, inverses)


def solution(mesh):
    in_specs = (
        P(None, "lev", "tile"),
        P(None, "tile"),
        P(None, None, "tile"),
        P("tile", None, None),
    )
    return jax.shard_map(
        per_device, mesh=mesh, in_specs=in_specs, out_specs=P(None, "lev", "tile"), check_vma=False
    )
```

```python
import functools

import jax
import jax.numpy as jnp
from jax import lax
from jax.experimental import pallas as pl
from jax.experimental.pallas import tpu as pltpu
from jax.sharding import PartitionSpec as P

SUBSTEPS = 3
NB = 4
HALO = 128
NY = 4
BLOCK = 256
LAG = 4
TAIL = 3
AHEAD = 4
F32, BF16 = jnp.float32, jnp.bfloat16
C = 0.4 * 0.5


def split(x):
    high = x.astype(BF16)
    return high, (x - high.astype(F32)).astype(BF16)


def dot(a, b):
    return jnp.dot(a, b, preferred_element_type=F32)


def kernel(prog, nbrs, metr, inv, out, X, PP, RS, RR, PB, PQ, M, IV, NBV, MTV, IH, IL,
           lsem, yin_s, yin_r, yin_l, out_s, out_r, out_l, z_s, z_r, b_s, b_r, h_s, h_r, e_s, e_r, e_l):
    lev, tile = lax.axis_index("lev"), lax.axis_index("tile")
    zh, y = lev // NY, lev % NY
    tiles = lax.axis_size("tile")
    half = X.shape[2]
    rows16 = half // NY
    slab = PP.shape[2]
    blocks = slab // BLOCK
    total = SUBSTEPS * blocks
    cell_count = prog.shape[2]

    def at(yy, tt):
        return {"lev": zh * NY + yy, "tile": tt}

    peers = [at((y + d) % NY, tile) for d in range(NY)]
    partner = {"lev": (1 - zh) * NY + y, "tile": tile}
    right = at((y + 1) % NY, (tile + jnp.where(y == NY - 1, 1, 0)) % tiles)
    left = at((y + NY - 1) % NY, (tile + jnp.where(y == 0, tiles - 1, 0)) % tiles)

    def remote(src, dst, ssem, rsem, dev):
        return pltpu.make_async_remote_copy(src, dst, ssem, rsem, device_id=dev, device_id_type=pl.DeviceIdType.MESH)

    def order(s, i):
        one = jnp.where(i < blocks - 2, i + 1, jnp.where(i == blocks - 2, 0, blocks - 1))
        two = jnp.where(i < blocks - 4, i + 2, jnp.where(i == blocks - 4, 1, jnp.where(i == blocks - 3, blocks - 2, one)))
        return jnp.where(s == 0, i, jnp.where(s == 1, one, two))

    def cells(c):
        return pl.ds(pl.multiple_of(HALO + c * BLOCK, 128), BLOCK)

    def lanes(c):
        return pl.ds(pl.multiple_of(c * BLOCK, 128), BLOCK)

    def y_in(c, d, last):
        yy = (y + d) % NY
        from_cell, count = c * BLOCK + HALO, BLOCK
        if last:
            count = BLOCK - HALO
        if isinstance(c, int) and c == 0:
            from_cell, count = 0, BLOCK + HALO
        parts = (
            (pl.ds(0, 3), from_cell, count),
            (pl.ds(3, 1), c * BLOCK, BLOCK),
        )
        copies = []
        for k, (fields, cell, width) in enumerate(parts):
            src = prog.at[fields, :, pl.ds(pl.multiple_of(yy * slab + cell, 128), width)]
            dst = X.at[0, fields, pl.ds(pl.multiple_of(y * rows16, 8), rows16), pl.ds(pl.multiple_of(HALO + cell, 128), width)]
            if d == 0:
                copies.append(pltpu.make_async_copy(src, dst, yin_l.at[k, c]))
            else:
                copies.append(remote(src, dst, yin_s.at[k, c, d - 1], yin_r.at[k, c, d - 1], peers[d]))
        return copies

    def y_in_each(c, what):
        if isinstance(c, int):
            what(c, c == blocks - 1)
        else:
            pl.when((c > 0) & (c < blocks - 1))(lambda: what(c, False))
            pl.when(c == blocks - 1)(lambda: what(blocks - 1, True))

    def y_in_start(c):
        def start(c, last):
            for d in range(NY):
                for copy in y_in(c, d, last):
                    copy.start()

        y_in_each(c, start)

    def y_in_wait(c):
        def wait(c, last):
            for copy in y_in(c, 0, last):
                copy.wait()
            for d in range(1, NY):
                for copy in y_in(c, d, last):
                    copy.wait_recv()

        y_in_each(c, wait)

    def y_in_sent(c):
        def sent(c, last):
            for d in range(1, NY):
                for copy in y_in(c, d, last):
                    copy.wait_send()

        y_in_each(c, sent)

    def edge(side, d, local=False):
        yy = (y + d) % NY
        own = pl.multiple_of(y * rows16, 8)
        if side == 0:
            first, put = (yy * slab + cell_count - HALO) % cell_count, 0
            dev = at(yy, (tile + jnp.where(yy == 0, 1, 0)) % tiles)
        else:
            first, put = ((yy + 1) * slab) % cell_count, HALO + slab
            dev = at(yy, (tile + jnp.where(yy == NY - 1, tiles - 1, 0)) % tiles)
        src = prog.at[pl.ds(0, 3), :, pl.ds(pl.multiple_of(first, 128), HALO)]
        dst = X.at[0, pl.ds(0, 3), pl.ds(own, rows16), pl.ds(put, HALO)]
        if local:
            return pltpu.make_async_copy(src, dst, e_l.at[side])
        return remote(src, dst, e_s.at[side, d], e_r.at[side, d], dev)

    outer = (0, NY - 1)

    def edge_start(side):
        for d in range(1, NY):
            edge(side, d).start()
        pl.when(y == outer[side])(lambda: edge(side, 0).start())
        pl.when(y != outer[side])(lambda: edge(side, 0, True).start())

    def edge_wait(side):
        for d in range(1, NY):
            edge(side, d).wait_recv()
        pl.when(y == outer[side])(lambda: edge(side, 0).wait_recv())
        pl.when(y != outer[side])(lambda: edge(side, 0, True).wait())

    def edge_drain(side):
        for d in range(1, NY):
            edge(side, d).wait_send()
        pl.when(y == outer[side])(lambda: edge(side, 0).wait_send())

    def y_out(f, c, d):
        yy = (y + d) % NY
        src = X.at[SUBSTEPS, pl.ds(2 * f, 2), pl.ds(pl.multiple_of(yy * rows16, 8), rows16), cells(c)]
        dst = out.at[pl.ds(2 * f, 2), :, pl.ds(pl.multiple_of(y * slab + c * BLOCK, 128), BLOCK)]
        if d == 0:
            return pltpu.make_async_copy(src, dst, out_l.at[f, c])
        return remote(src, dst, out_s.at[f, c, d - 1], out_r.at[f, c, d - 1], peers[d])

    def y_out_wait(f, c):
        for d in range(NY):
            y_out(f, c, d).wait()

    def z_copies(s, c):
        return (
            remote(RS.at[s, :, lanes(c)], RR.at[s, :, lanes(c)], z_s.at[s, c], z_r.at[s, c], partner),
            remote(PB.at[s, c], PQ.at[s, c], b_s.at[s, c], b_r.at[s, c], partner),
        )

    def halo(s, side):
        if side == 0:
            src, dst, dev = pl.ds(HALO, HALO), pl.ds(HALO + slab, HALO), left
        else:
            src, dst, dev = pl.ds(slab, HALO), pl.ds(0, HALO), right
        return remote(X.at[s, pl.ds(0, 3), :, src], X.at[s, pl.ds(0, 3), :, dst], h_s.at[s, side], h_r.at[s, side], dev)

    barrier = pltpu.get_barrier_semaphore()
    others = peers[1:] + [partner, left, right]
    for dev in others:
        pl.semaphore_signal(barrier, 1, device_id=dev, device_id_type=pl.DeviceIdType.MESH)
    for side in range(2):
        @pl.when(y == outer[side])
        def _():
            for yy in range(NY):
                dev = at(yy, (tile + (1 if side else tiles - 1)) % tiles)
                pl.semaphore_signal(barrier, 1, device_id=dev, device_id_type=pl.DeviceIdType.MESH)

    local = (
        pltpu.make_async_copy(nbrs.at[:, pl.ds(pl.multiple_of(y * slab, 128), slab)], NBV, lsem.at[0]),
        pltpu.make_async_copy(metr.at[:, :, pl.ds(pl.multiple_of(y * slab, 128), slab)], MTV, lsem.at[1]),
    )
    local = local + (pltpu.make_async_copy(inv.at[0], IV, lsem.at[2]),)
    for copy in local:
        copy.start()
    pl.semaphore_wait(barrier, len(others) + 2)
    edge_start(0)
    for c in range(AHEAD):
        y_in_start(c)
    edge_start(1)
    for copy in local:
        copy.wait()

    full = IV[...]
    swapped = jnp.where(zh == 0, full, pltpu.roll(full, half, 1))
    mine = jnp.concatenate([
        jnp.where(zh == 0, swapped[:half], swapped[half:]),
        jnp.where(zh == 0, swapped[half:half + 8], swapped[half - 8:half]),
    ])
    IH[...], IL[...] = split(mine)

    level = lax.broadcasted_iota(jnp.int32, (half, BLOCK), 0)
    first, last = level == 0, level == half - 1

    def build(c):
        def rows(j, carry):
            r0 = pl.multiple_of(j * 64, 64)
            slot = lax.broadcasted_iota(jnp.int32, (64, BLOCK), 0) + r0
            cell = lax.broadcasted_iota(jnp.int32, (64, BLOCK), 1)
            here = slot == cell + HALO
            m0 = jnp.zeros((64, BLOCK), F32)
            m1 = jnp.zeros((64, BLOCK), F32)
            for k in range(NB):
                w0, w1 = MTV[0, pl.ds(k, 1), lanes(c)], MTV[1, pl.ds(k, 1), lanes(c)]
                hit = slot == NBV[pl.ds(k, 1), lanes(c)] - (y * slab + c * BLOCK)
                m0 = m0 + (jnp.where(hit, w0, 0.0) - jnp.where(here, w0, 0.0))
                m1 = m1 + (jnp.where(hit, w1, 0.0) - jnp.where(here, w1, 0.0))
            M[c, 0, pl.ds(r0, 64), :], M[c, 1, pl.ds(r0, 64), :] = split(m0)
            M[c, 2, pl.ds(r0, 64), :], M[c, 3, pl.ds(r0, 64), :] = split(m1)
            return carry

        lax.fori_loop(0, (BLOCK + 2 * HALO) // 64, rows, 0)

    def horizontal(s, c):
        window = pl.ds(pl.multiple_of(c * BLOCK, 128), BLOCK + 2 * HALO)
        uh, ul = split(X[s, 0, :, window])
        vh, vl = split(X[s, 1, :, window])
        ph, pl_ = split(X[s, 2, :, window])
        a0 = dot(jnp.concatenate([ph, uh, pl_, ul]), M[c, 0])
        b0 = dot(jnp.concatenate([ph, uh]), M[c, 1])
        a1 = dot(jnp.concatenate([ph, vh, pl_, vl]), M[c, 2])
        b1 = dot(jnp.concatenate([ph, vh]), M[c, 3])
        g0 = a0[: 2 * half] + a0[2 * half :] + b0
        g1 = a1[: 2 * half] + a1[2 * half :] + b1
        X[s + 1, 0, :, cells(c)] = X[s, 0, :, cells(c)] - g0[:half]
        X[s + 1, 1, :, cells(c)] = X[s, 1, :, cells(c)] - g1[:half]
        p = X[s, 2, :, cells(c)] - (g0[half:] + g1[half:])
        PP[s, :, lanes(c)] = p
        up = jnp.where(last, 0.0, pltpu.roll(p, half - 1, 0))
        down = jnp.where(first, 0.0, pltpu.roll(p, 1, 0))
        RS[s, :, lanes(c)] = X[s, 3, :, cells(c)] - C * (up - down)
        PB[s, c] = jnp.where(zh == 0, p[half - 1 :], p[:1])

    def vertical(s, c):
        top = jnp.where(zh == 0, 1.0, 0.0)
        own_b, other_b = PB[s, c], PQ[s, c]
        fix_own = jnp.where(last, -C * top, 0.0) + jnp.where(first, C * (1.0 - top), 0.0)
        fix_other = jnp.where(first, C * top, 0.0) + jnp.where(last, -C * (1.0 - top), 0.0)
        own = RS[s, :, lanes(c)] + fix_own * other_b
        other = RR[s, :, lanes(c)] + fix_other * own_b
        rh, rl = split(jnp.concatenate([own, other]))
        ih, il = IH[...], IL[...]
        w = dot(ih, rh) + (dot(ih, rl) + dot(il, rh))
        edge = jnp.where(zh == 0, w[half : half + 1], w[half + 7 : half + 8])
        w = w[:half]
        up = jnp.where(last, edge * top, pltpu.roll(w, half - 1, 0))
        down = jnp.where(first, edge * (1.0 - top), pltpu.roll(w, 1, 0))
        X[s + 1, 2, :, cells(c)] = PP[s, :, lanes(c)] - C * (up - down)
        X[s + 1, 3, :, cells(c)] = w

    def finish(t):
        s, c = t // blocks, order(t // blocks, t % blocks)
        for copy in z_copies(s, c):
            copy.wait()
        vertical(s, c)

        @pl.when((s < SUBSTEPS - 1) & (c == 0))
        def _():
            halo(s + 1, 0).start()

        @pl.when((s < SUBSTEPS - 1) & (c == blocks - 1))
        def _():
            halo(s + 1, 1).start()

        @pl.when(s == SUBSTEPS - 1)
        def _():
            for d in range(NY):
                y_out(1, c, d).start()
            y_out_wait(0, c)

            @pl.when(t % blocks >= TAIL)
            def _():
                y_out_wait(1, order(s, t % blocks - TAIL))

    def begin(t):
        s, i = t // blocks, t % blocks
        c = order(s, i)

        @pl.when(s == 0)
        def _():
            build(c)

            @pl.when(i == 0)
            def _():
                edge_wait(0)
                y_in_wait(0)

            y_in_wait(i)

            @pl.when(i == blocks - 1)
            def _():
                edge_wait(1)

            @pl.when(i + AHEAD < blocks)
            def _():
                y_in_start(i + AHEAD)

        @pl.when(s == 1)
        def _():
            pl.when(i == 0)(lambda: y_in_sent(0))
            y_in_sent(i)

        @pl.when((s > 0) & (c == 0))
        def _():
            halo(s, 1).wait_recv()

        @pl.when((s > 0) & (c == blocks - 1))
        def _():
            halo(s, 0).wait_recv()

        horizontal(s, c)
        for copy in z_copies(s, c):
            copy.start()

        @pl.when(s == SUBSTEPS - 1)
        def _():
            for d in range(NY):
                y_out(0, c, d).start()

    def step(t, carry):
        @pl.when(t >= LAG)
        def _():
            finish(t - LAG)

        @pl.when(t < total)
        def _():
            begin(t)

        @pl.when(t == total)
        def _():
            for side in range(2):
                edge_drain(side)
                for s in range(1, SUBSTEPS):
                    halo(s, side).wait_send()

        return carry

    lax.fori_loop(0, total + LAG, step, 0)

    for i in range(blocks - TAIL, blocks):
        y_out_wait(1, order(SUBSTEPS - 1, i))


def per_device(prognostic, neighbours, metric, inverses):
    fields, rows16, cell_count = prognostic.shape
    half, slab = rows16 * NY, cell_count // NY
    blocks = slab // BLOCK
    dma = pltpu.SemaphoreType.DMA
    anywhere = pl.BlockSpec(memory_space=pltpu.HBM)
    return pl.pallas_call(
        kernel,
        name="acoustic",
        out_shape=jax.ShapeDtypeStruct(prognostic.shape, F32),
        in_specs=[anywhere, anywhere, anywhere, anywhere],
        out_specs=anywhere,
        scratch_shapes=[
            pltpu.VMEM((SUBSTEPS + 1, fields, half, slab + 2 * HALO), F32),
            pltpu.VMEM((SUBSTEPS, half, slab), F32),
            pltpu.VMEM((SUBSTEPS, half, slab), F32),
            pltpu.VMEM((SUBSTEPS, half, slab), F32),
            pltpu.VMEM((SUBSTEPS, blocks, 1, BLOCK), F32),
            pltpu.VMEM((SUBSTEPS, blocks, 1, BLOCK), F32),
            pltpu.VMEM((blocks, 4, BLOCK + 2 * HALO, BLOCK), BF16),
            pltpu.VMEM((2 * half, 2 * half), F32),
            pltpu.VMEM((NB, slab), jnp.int32),
            pltpu.VMEM((2, NB, slab), F32),
            pltpu.VMEM((half + 8, 2 * half), BF16),
            pltpu.VMEM((half + 8, 2 * half), BF16),
            dma((3,)),
            dma((2, blocks, NY - 1)),
            dma((2, blocks, NY - 1)),
            dma((2, blocks)),
            dma((2, blocks, NY - 1)),
            dma((2, blocks, NY - 1)),
            dma((2, blocks)),
            dma((SUBSTEPS, blocks)),
            dma((SUBSTEPS, blocks)),
            dma((SUBSTEPS, blocks)),
            dma((SUBSTEPS, blocks)),
            dma((SUBSTEPS, 2)),
            dma((SUBSTEPS, 2)),
            dma((2, NY)),
            dma((2, NY)),
            dma((2,)),
        ],
        compiler_params=pltpu.CompilerParams(
            collective_id=0, has_side_effects=True, vmem_limit_bytes=62 << 20
        ),
    )(prognostic, neighbours, metric, inverses)


def solution(mesh):
    in_specs = (
        P(None, "lev", "tile"),
        P(None, "tile"),
        P(None, None, "tile"),
        P("tile", None, None),
    )
    return jax.shard_map(
        per_device, mesh=mesh, in_specs=in_specs, out_specs=P(None, "lev", "tile"), check_vma=False
    )
```

```python
import functools

import jax
import jax.numpy as jnp
from jax import lax
from jax.experimental import pallas as pl
from jax.experimental.pallas import tpu as pltpu
from jax.sharding import PartitionSpec as P

SUBSTEPS = 3
NB = 4
HALO = 128
NY = 4
BLOCK = 256
LAG = 4
TAIL = 3
AHEAD = 4
F32, BF16 = jnp.float32, jnp.bfloat16
C = 0.4 * 0.5


def split(x):
    high = x.astype(BF16)
    return high, (x - high.astype(F32)).astype(BF16)


def dot(a, b):
    return jnp.dot(a, b, preferred_element_type=F32)


def kernel(prog, nbrs, metr, inv, out, X, PP, RS, RR, PB, PQ, M, IV, NBV, MTV, IH, IL,
           lsem, yin_s, yin_r, yin_l, out_s, out_r, out_l, z_s, z_r, b_s, b_r, h_s, h_r, e_s, e_r, e_l):
    lev, tile = lax.axis_index("lev"), lax.axis_index("tile")
    zh, y = lev // NY, lev % NY
    tiles = lax.axis_size("tile")
    half = X.shape[2]
    rows16 = half // NY
    slab = PP.shape[2]
    blocks = slab // BLOCK
    total = SUBSTEPS * blocks
    cell_count = prog.shape[2]

    def at(yy, tt):
        return {"lev": zh * NY + yy, "tile": tt}

    peers = [at((y + d) % NY, tile) for d in range(NY)]
    partner = {"lev": (1 - zh) * NY + y, "tile": tile}
    right = at((y + 1) % NY, (tile + jnp.where(y == NY - 1, 1, 0)) % tiles)
    left = at((y + NY - 1) % NY, (tile + jnp.where(y == 0, tiles - 1, 0)) % tiles)

    def remote(src, dst, ssem, rsem, dev):
        return pltpu.make_async_remote_copy(src, dst, ssem, rsem, device_id=dev, device_id_type=pl.DeviceIdType.MESH)

    def order(s, i):
        one = jnp.where(i < blocks - 2, i + 1, jnp.where(i == blocks - 2, 0, blocks - 1))
        two = jnp.where(i < blocks - 4, i + 2, jnp.where(i == blocks - 4, 1, jnp.where(i == blocks - 3, blocks - 2, one)))
        return jnp.where(s == 0, i, jnp.where(s == 1, one, two))

    def cells(c):
        return pl.ds(pl.multiple_of(HALO + c * BLOCK, 128), BLOCK)

    def lanes(c):
        return pl.ds(pl.multiple_of(c * BLOCK, 128), BLOCK)

    def y_in(c, d, last):
        yy = (y + d) % NY
        from_cell, count = c * BLOCK + HALO, BLOCK
        if last:
            count = BLOCK - HALO
        if isinstance(c, int) and c == 0:
            from_cell, count = 0, BLOCK + HALO
        parts = (
            (pl.ds(0, 3), from_cell, count),
            (pl.ds(3, 1), c * BLOCK, BLOCK),
        )
        copies = []
        for k, (fields, cell, width) in enumerate(parts):
            src = prog.at[fields, :, pl.ds(pl.multiple_of(yy * slab + cell, 128), width)]
            dst = X.at[0, fields, pl.ds(pl.multiple_of(y * rows16, 8), rows16), pl.ds(pl.multiple_of(HALO + cell, 128), width)]
            if d == 0:
                copies.append(pltpu.make_async_copy(src, dst, yin_l.at[k, c]))
            else:
                copies.append(remote(src, dst, yin_s.at[k, c, d - 1], yin_r.at[k, c, d - 1], peers[d]))
        return copies

    def y_in_each(c, what):
        if isinstance(c, int):
            what(c, c == blocks - 1)
        else:
            pl.when((c > 0) & (c < blocks - 1))(lambda: what(c, False))
            pl.when(c == blocks - 1)(lambda: what(blocks - 1, True))

    def y_in_start(c):
        def start(c, last):
            for d in range(NY):
                for copy in y_in(c, d, last):
                    copy.start()

        y_in_each(c, start)

    def y_in_wait(c):
        def wait(c, last):
            for copy in y_in(c, 0, last):
                copy.wait()
            for d in range(1, NY):
                for copy in y_in(c, d, last):
                    copy.wait_recv()

        y_in_each(c, wait)

    def y_in_sent(c):
        def sent(c, last):
            for d in range(1, NY):
                for copy in y_in(c, d, last):
                    copy.wait_send()

        y_in_each(c, sent)

    def edge(side, d, local=False):
        yy = (y + d) % NY
        own = pl.multiple_of(y * rows16, 8)
        if side == 0:
            first, put = (yy * slab + cell_count - HALO) % cell_count, 0
            dev = at(yy, (tile + jnp.where(yy == 0, 1, 0)) % tiles)
        else:
            first, put = ((yy + 1) * slab) % cell_count, HALO + slab
            dev = at(yy, (tile + jnp.where(yy == NY - 1, tiles - 1, 0)) % tiles)
        src = prog.at[pl.ds(0, 3), :, pl.ds(pl.multiple_of(first, 128), HALO)]
        dst = X.at[0, pl.ds(0, 3), pl.ds(own, rows16), pl.ds(put, HALO)]
        if local:
            return pltpu.make_async_copy(src, dst, e_l.at[side])
        return remote(src, dst, e_s.at[side, d], e_r.at[side, d], dev)

    outer = (0, NY - 1)

    def edge_start(side):
        for d in range(1, NY):
            edge(side, d).start()
        pl.when(y == outer[side])(lambda: edge(side, 0).start())
        pl.when(y != outer[side])(lambda: edge(side, 0, True).start())

    def edge_wait(side):
        for d in range(1, NY):
            edge(side, d).wait_recv()
        pl.when(y == outer[side])(lambda: edge(side, 0).wait_recv())
        pl.when(y != outer[side])(lambda: edge(side, 0, True).wait())

    def edge_drain(side):
        for d in range(1, NY):
            edge(side, d).wait_send()
        pl.when(y == outer[side])(lambda: edge(side, 0).wait_send())

    def y_out(f, c, d):
        yy = (y + d) % NY
        src = X.at[SUBSTEPS, pl.ds(2 * f, 2), pl.ds(pl.multiple_of(yy * rows16, 8), rows16), cells(c)]
        dst = out.at[pl.ds(2 * f, 2), :, pl.ds(pl.multiple_of(y * slab + c * BLOCK, 128), BLOCK)]
        if d == 0:
            return pltpu.make_async_copy(src, dst, out_l.at[f, c])
        return remote(src, dst, out_s.at[f, c, d - 1], out_r.at[f, c, d - 1], peers[d])

    def y_out_wait(f, c):
        for d in range(NY):
            y_out(f, c, d).wait()

    def z_copies(s, c):
        return (
            remote(RS.at[s, :, lanes(c)], RR.at[s, :, lanes(c)], z_s.at[s, c], z_r.at[s, c], partner),
            remote(PB.at[s, c], PQ.at[s, c], b_s.at[s, c], b_r.at[s, c], partner),
        )

    def halo(s, side):
        if side == 0:
            src, dst, dev = pl.ds(HALO, HALO), pl.ds(HALO + slab, HALO), left
        else:
            src, dst, dev = pl.ds(slab, HALO), pl.ds(0, HALO), right
        return remote(X.at[s, pl.ds(0, 3), :, src], X.at[s, pl.ds(0, 3), :, dst], h_s.at[s, side], h_r.at[s, side], dev)

    barrier = pltpu.get_barrier_semaphore()
    others = peers[1:] + [partner, left, right]
    for dev in others:
        pl.semaphore_signal(barrier, 1, device_id=dev, device_id_type=pl.DeviceIdType.MESH)
    for side in range(2):
        @pl.when(y == outer[side])
        def _():
            for yy in range(NY):
                dev = at(yy, (tile + (1 if side else tiles - 1)) % tiles)
                pl.semaphore_signal(barrier, 1, device_id=dev, device_id_type=pl.DeviceIdType.MESH)

    local = (
        pltpu.make_async_copy(nbrs.at[:, pl.ds(pl.multiple_of(y * slab, 128), slab)], NBV, lsem.at[0]),
        pltpu.make_async_copy(metr.at[:, :, pl.ds(pl.multiple_of(y * slab, 128), slab)], MTV, lsem.at[1]),
    )
    local = local + (pltpu.make_async_copy(inv.at[0], IV, lsem.at[2]),)
    for copy in local:
        copy.start()
    pl.semaphore_wait(barrier, len(others) + 2)
    edge_start(0)
    for c in range(AHEAD):
        y_in_start(c)
    for copy in local:
        copy.wait()

    full = IV[...]
    swapped = jnp.where(zh == 0, full, pltpu.roll(full, half, 1))
    mine = jnp.concatenate([
        jnp.where(zh == 0, swapped[:half], swapped[half:]),
        jnp.where(zh == 0, swapped[half:half + 8], swapped[half - 8:half]),
    ])
    IH[...], IL[...] = split(mine)

    level = lax.broadcasted_iota(jnp.int32, (half, BLOCK), 0)
    first, last = level == 0, level == half - 1

    def build(c):
        def rows(j, carry):
            r0 = pl.multiple_of(j * 64, 64)
            slot = lax.broadcasted_iota(jnp.int32, (64, BLOCK), 0) + r0
            cell = lax.broadcasted_iota(jnp.int32, (64, BLOCK), 1)
            here = slot == cell + HALO
            m0 = jnp.zeros((64, BLOCK), F32)
            m1 = jnp.zeros((64, BLOCK), F32)
            for k in range(NB):
                w0, w1 = MTV[0, pl.ds(k, 1), lanes(c)], MTV[1, pl.ds(k, 1), lanes(c)]
                hit = slot == NBV[pl.ds(k, 1), lanes(c)] - (y * slab + c * BLOCK)
                m0 = m0 + (jnp.where(hit, w0, 0.0) - jnp.where(here, w0, 0.0))
                m1 = m1 + (jnp.where(hit, w1, 0.0) - jnp.where(here, w1, 0.0))
            M[c, 0, pl.ds(r0, 64), :], M[c, 1, pl.ds(r0, 64), :] = split(m0)
            M[c, 2, pl.ds(r0, 64), :], M[c, 3, pl.ds(r0, 64), :] = split(m1)
            return carry

        lax.fori_loop(0, (BLOCK + 2 * HALO) // 64, rows, 0)

    def horizontal(s, c):
        window = pl.ds(pl.multiple_of(c * BLOCK, 128), BLOCK + 2 * HALO)
        uh, ul = split(X[s, 0, :, window])
        vh, vl = split(X[s, 1, :, window])
        ph, pl_ = split(X[s, 2, :, window])
        a0 = dot(jnp.concatenate([ph, uh, pl_, ul]), M[c, 0])
        b0 = dot(jnp.concatenate([ph, uh]), M[c, 1])
        a1 = dot(jnp.concatenate([ph, vh, pl_, vl]), M[c, 2])
        b1 = dot(jnp.concatenate([ph, vh]), M[c, 3])
        g0 = a0[: 2 * half] + a0[2 * half :] + b0
        g1 = a1[: 2 * half] + a1[2 * half :] + b1
        X[s + 1, 0, :, cells(c)] = X[s, 0, :, cells(c)] - g0[:half]
        X[s + 1, 1, :, cells(c)] = X[s, 1, :, cells(c)] - g1[:half]
        p = X[s, 2, :, cells(c)] - (g0[half:] + g1[half:])
        PP[s, :, lanes(c)] = p
        up = jnp.where(last, 0.0, pltpu.roll(p, half - 1, 0))
        down = jnp.where(first, 0.0, pltpu.roll(p, 1, 0))
        RS[s, :, lanes(c)] = X[s, 3, :, cells(c)] - C * (up - down)
        PB[s, c] = jnp.where(zh == 0, p[half - 1 :], p[:1])

    def vertical(s, c):
        top = jnp.where(zh == 0, 1.0, 0.0)
        own_b, other_b = PB[s, c], PQ[s, c]
        fix_own = jnp.where(last, -C * top, 0.0) + jnp.where(first, C * (1.0 - top), 0.0)
        fix_other = jnp.where(first, C * top, 0.0) + jnp.where(last, -C * (1.0 - top), 0.0)
        own = RS[s, :, lanes(c)] + fix_own * other_b
        other = RR[s, :, lanes(c)] + fix_other * own_b
        rh, rl = split(jnp.concatenate([own, other]))
        ih, il = IH[...], IL[...]
        w = dot(ih, rh) + (dot(ih, rl) + dot(il, rh))
        edge = jnp.where(zh == 0, w[half : half + 1], w[half + 7 : half + 8])
        w = w[:half]
        up = jnp.where(last, edge * top, pltpu.roll(w, half - 1, 0))
        down = jnp.where(first, edge * (1.0 - top), pltpu.roll(w, 1, 0))
        X[s + 1, 2, :, cells(c)] = PP[s, :, lanes(c)] - C * (up - down)
        X[s + 1, 3, :, cells(c)] = w

    def finish(t):
        s, c = t // blocks, order(t // blocks, t % blocks)
        for copy in z_copies(s, c):
            copy.wait()
        vertical(s, c)

        @pl.when((s < SUBSTEPS - 1) & (c == 0))
        def _():
            halo(s + 1, 0).start()

        @pl.when((s < SUBSTEPS - 1) & (c == blocks - 1))
        def _():
            halo(s + 1, 1).start()

        @pl.when(s == SUBSTEPS - 1)
        def _():
            for d in range(NY):
                y_out(1, c, d).start()
            y_out_wait(0, c)

            @pl.when(t % blocks >= TAIL)
            def _():
                y_out_wait(1, order(s, t % blocks - TAIL))

    def begin(t):
        s, i = t // blocks, t % blocks
        c = order(s, i)

        @pl.when(s == 0)
        def _():
            build(c)

            @pl.when(i == 0)
            def _():
                edge_wait(0)
                y_in_wait(0)

            y_in_wait(i)

            @pl.when(i == blocks - 1)
            def _():
                edge_wait(1)

            @pl.when(i + AHEAD < blocks)
            def _():
                y_in_start(i + AHEAD)

            @pl.when(i == 3)
            def _():
                edge_start(1)

        @pl.when(s == 1)
        def _():
            pl.when(i == 0)(lambda: y_in_sent(0))
            y_in_sent(i)

        @pl.when((s > 0) & (c == 0))
        def _():
            halo(s, 1).wait_recv()

        @pl.when((s > 0) & (c == blocks - 1))
        def _():
            halo(s, 0).wait_recv()

        horizontal(s, c)
        for copy in z_copies(s, c):
            copy.start()

        @pl.when(s == SUBSTEPS - 1)
        def _():
            for d in range(NY):
                y_out(0, c, d).start()

    def step(t, carry):
        @pl.when(t >= LAG)
        def _():
            finish(t - LAG)

        @pl.when(t < total)
        def _():
            begin(t)

        @pl.when(t == total)
        def _():
            for side in range(2):
                edge_drain(side)
                for s in range(1, SUBSTEPS):
                    halo(s, side).wait_send()

        return carry

    lax.fori_loop(0, total + LAG, step, 0)

    for i in range(blocks - TAIL, blocks):
        y_out_wait(1, order(SUBSTEPS - 1, i))


def per_device(prognostic, neighbours, metric, inverses):
    fields, rows16, cell_count = prognostic.shape
    half, slab = rows16 * NY, cell_count // NY
    blocks = slab // BLOCK
    dma = pltpu.SemaphoreType.DMA
    anywhere = pl.BlockSpec(memory_space=pltpu.HBM)
    return pl.pallas_call(
        kernel,
        name="acoustic",
        out_shape=jax.ShapeDtypeStruct(prognostic.shape, F32),
        in_specs=[anywhere, anywhere, anywhere, anywhere],
        out_specs=anywhere,
        scratch_shapes=[
            pltpu.VMEM((SUBSTEPS + 1, fields, half, slab + 2 * HALO), F32),
            pltpu.VMEM((SUBSTEPS, half, slab), F32),
            pltpu.VMEM((SUBSTEPS, half, slab), F32),
            pltpu.VMEM((SUBSTEPS, half, slab), F32),
            pltpu.VMEM((SUBSTEPS, blocks, 1, BLOCK), F32),
            pltpu.VMEM((SUBSTEPS, blocks, 1, BLOCK), F32),
            pltpu.VMEM((blocks, 4, BLOCK + 2 * HALO, BLOCK), BF16),
            pltpu.VMEM((2 * half, 2 * half), F32),
            pltpu.VMEM((NB, slab), jnp.int32),
            pltpu.VMEM((2, NB, slab), F32),
            pltpu.VMEM((half + 8, 2 * half), BF16),
            pltpu.VMEM((half + 8, 2 * half), BF16),
            dma((3,)),
            dma((2, blocks, NY - 1)),
            dma((2, blocks, NY - 1)),
            dma((2, blocks)),
            dma((2, blocks, NY - 1)),
            dma((2, blocks, NY - 1)),
            dma((2, blocks)),
            dma((SUBSTEPS, blocks)),
            dma((SUBSTEPS, blocks)),
            dma((SUBSTEPS, blocks)),
            dma((SUBSTEPS, blocks)),
            dma((SUBSTEPS, 2)),
            dma((SUBSTEPS, 2)),
            dma((2, NY)),
            dma((2, NY)),
            dma((2,)),
        ],
        compiler_params=pltpu.CompilerParams(
            collective_id=0, has_side_effects=True, vmem_limit_bytes=62 << 20
        ),
    )(prognostic, neighbours, metric, inverses)


def solution(mesh):
    in_specs = (
        P(None, "lev", "tile"),
        P(None, "tile"),
        P(None, None, "tile"),
        P("tile", None, None),
    )
    return jax.shard_map(
        per_device, mesh=mesh, in_specs=in_specs, out_specs=P(None, "lev", "tile"), check_vma=False
    )
```

```python
import functools

import jax
import jax.numpy as jnp
from jax import lax
from jax.experimental import pallas as pl
from jax.experimental.pallas import tpu as pltpu
from jax.sharding import PartitionSpec as P

SUBSTEPS = 3
NB = 4
HALO = 128
NY = 4
BLOCK = 256
LAG = 4
TAIL = 3
AHEAD = 4
F32, BF16 = jnp.float32, jnp.bfloat16
C = 0.4 * 0.5


def split(x):
    high = x.astype(BF16)
    return high, (x - high.astype(F32)).astype(BF16)


def dot(a, b):
    return jnp.dot(a, b, preferred_element_type=F32)


def kernel(prog, nbrs, metr, inv, out, X, PP, RS, RR, PB, PQ, M, IV, NBV, MTV, IH, IL,
           lsem, yin_s, yin_r, yin_l, out_s, out_r, out_l, z_s, z_r, b_s, b_r, h_s, h_r, e_s, e_r, e_l):
    lev, tile = lax.axis_index("lev"), lax.axis_index("tile")
    zh, y = lev // NY, lev % NY
    tiles = lax.axis_size("tile")
    half = X.shape[2]
    rows16 = half // NY
    slab = PP.shape[2]
    blocks = slab // BLOCK
    total = SUBSTEPS * blocks
    cell_count = prog.shape[2]

    def at(yy, tt):
        return {"lev": zh * NY + yy, "tile": tt}

    peers = [at((y + d) % NY, tile) for d in range(NY)]
    partner = {"lev": (1 - zh) * NY + y, "tile": tile}
    right = at((y + 1) % NY, (tile + jnp.where(y == NY - 1, 1, 0)) % tiles)
    left = at((y + NY - 1) % NY, (tile + jnp.where(y == 0, tiles - 1, 0)) % tiles)

    def remote(src, dst, ssem, rsem, dev):
        return pltpu.make_async_remote_copy(src, dst, ssem, rsem, device_id=dev, device_id_type=pl.DeviceIdType.MESH)

    def order(s, i):
        one = jnp.where(i < blocks - 2, i + 1, jnp.where(i == blocks - 2, 0, blocks - 1))
        two = jnp.where(i < blocks - 4, i + 2, jnp.where(i == blocks - 4, 1, jnp.where(i == blocks - 3, blocks - 2, one)))
        return jnp.where(s == 0, i, jnp.where(s == 1, one, two))

    def cells(c):
        return pl.ds(pl.multiple_of(HALO + c * BLOCK, 128), BLOCK)

    def lanes(c):
        return pl.ds(pl.multiple_of(c * BLOCK, 128), BLOCK)

    def y_in(c, d, last):
        yy = (y + d) % NY
        from_cell, count = c * BLOCK + HALO, BLOCK
        if last:
            count = BLOCK - HALO
        if isinstance(c, int) and c == 0:
            from_cell, count = 0, BLOCK + HALO
        parts = (
            (pl.ds(0, 3), from_cell, count),
            (pl.ds(3, 1), c * BLOCK, BLOCK),
        )
        copies = []
        for k, (fields, cell, width) in enumerate(parts):
            src = prog.at[fields, :, pl.ds(pl.multiple_of(yy * slab + cell, 128), width)]
            dst = X.at[0, fields, pl.ds(pl.multiple_of(y * rows16, 8), rows16), pl.ds(pl.multiple_of(HALO + cell, 128), width)]
            if d == 0:
                copies.append(pltpu.make_async_copy(src, dst, yin_l.at[k, c]))
            else:
                copies.append(remote(src, dst, yin_s.at[k, c, d - 1], yin_r.at[k, c, d - 1], peers[d]))
        return copies

    def y_in_each(c, what):
        if isinstance(c, int):
            what(c, c == blocks - 1)
        else:
            pl.when((c > 0) & (c < blocks - 1))(lambda: what(c, False))
            pl.when(c == blocks - 1)(lambda: what(blocks - 1, True))

    def y_in_start(c):
        def start(c, last):
            for d in range(NY):
                for copy in y_in(c, d, last):
                    copy.start()

        y_in_each(c, start)

    def y_in_wait(c):
        def wait(c, last):
            for copy in y_in(c, 0, last):
                copy.wait()
            for d in range(1, NY):
                for copy in y_in(c, d, last):
                    copy.wait_recv()

        y_in_each(c, wait)

    def y_in_sent(c):
        def sent(c, last):
            for d in range(1, NY):
                for copy in y_in(c, d, last):
                    copy.wait_send()

        y_in_each(c, sent)

    def edge(side, d, local=False):
        yy = (y + d) % NY
        own = pl.multiple_of(y * rows16, 8)
        if side == 0:
            first, put = (yy * slab + cell_count - HALO) % cell_count, 0
            dev = at(yy, (tile + jnp.where(yy == 0, 1, 0)) % tiles)
        else:
            first, put = ((yy + 1) * slab) % cell_count, HALO + slab
            dev = at(yy, (tile + jnp.where(yy == NY - 1, tiles - 1, 0)) % tiles)
        src = prog.at[pl.ds(0, 3), :, pl.ds(pl.multiple_of(first, 128), HALO)]
        dst = X.at[0, pl.ds(0, 3), pl.ds(own, rows16), pl.ds(put, HALO)]
        if local:
            return pltpu.make_async_copy(src, dst, e_l.at[side])
        return remote(src, dst, e_s.at[side, d], e_r.at[side, d], dev)

    outer = (0, NY - 1)

    def edge_start(side):
        for d in range(1, NY):
            edge(side, d).start()
        pl.when(y == outer[side])(lambda: edge(side, 0).start())
        pl.when(y != outer[side])(lambda: edge(side, 0, True).start())

    def edge_wait(side):
        for d in range(1, NY):
            edge(side, d).wait_recv()
        pl.when(y == outer[side])(lambda: edge(side, 0).wait_recv())
        pl.when(y != outer[side])(lambda: edge(side, 0, True).wait())

    def edge_drain(side):
        for d in range(1, NY):
            edge(side, d).wait_send()
        pl.when(y == outer[side])(lambda: edge(side, 0).wait_send())

    def y_out(f, c, d):
        yy = (y + d) % NY
        src = X.at[SUBSTEPS, pl.ds(2 * f, 2), pl.ds(pl.multiple_of(yy * rows16, 8), rows16), cells(c)]
        dst = out.at[pl.ds(2 * f, 2), :, pl.ds(pl.multiple_of(y * slab + c * BLOCK, 128), BLOCK)]
        if d == 0:
            return pltpu.make_async_copy(src, dst, out_l.at[f, c])
        return remote(src, dst, out_s.at[f, c, d - 1], out_r.at[f, c, d - 1], peers[d])

    def y_out_wait(f, c):
        for d in range(NY):
            y_out(f, c, d).wait()

    def z_copies(s, c):
        return (
            remote(RS.at[s, :, lanes(c)], RR.at[s, :, lanes(c)], z_s.at[s, c], z_r.at[s, c], partner),
            remote(PB.at[s, c], PQ.at[s, c], b_s.at[s, c], b_r.at[s, c], partner),
        )

    def halo(s, side):
        if side == 0:
            src, dst, dev = pl.ds(HALO, HALO), pl.ds(HALO + slab, HALO), left
        else:
            src, dst, dev = pl.ds(slab, HALO), pl.ds(0, HALO), right
        return remote(X.at[s, pl.ds(0, 3), :, src], X.at[s, pl.ds(0, 3), :, dst], h_s.at[s, side], h_r.at[s, side], dev)

    barrier = pltpu.get_barrier_semaphore()
    others = peers[1:] + [partner, left, right]
    for dev in others:
        pl.semaphore_signal(barrier, 1, device_id=dev, device_id_type=pl.DeviceIdType.MESH)
    for side in range(2):
        @pl.when(y == outer[side])
        def _():
            for yy in range(NY):
                dev = at(yy, (tile + (1 if side else tiles - 1)) % tiles)
                pl.semaphore_signal(barrier, 1, device_id=dev, device_id_type=pl.DeviceIdType.MESH)

    local = (
        pltpu.make_async_copy(nbrs.at[:, pl.ds(pl.multiple_of(y * slab, 128), slab)], NBV, lsem.at[0]),
        pltpu.make_async_copy(metr.at[:, :, pl.ds(pl.multiple_of(y * slab, 128), slab)], MTV, lsem.at[1]),
    )
    local = local + (pltpu.make_async_copy(inv.at[0], IV, lsem.at[2]),)
    for copy in local:
        copy.start()
    pl.semaphore_wait(barrier, len(others) + 2)
    y_in_start(0)
    edge_start(0)
    for c in range(1, AHEAD):
        y_in_start(c)
    for copy in local:
        copy.wait()

    full = IV[...]
    swapped = jnp.where(zh == 0, full, pltpu.roll(full, half, 1))
    mine = jnp.concatenate([
        jnp.where(zh == 0, swapped[:half], swapped[half:]),
        jnp.where(zh == 0, swapped[half:half + 8], swapped[half - 8:half]),
    ])
    IH[...], IL[...] = split(mine)

    level = lax.broadcasted_iota(jnp.int32, (half, BLOCK), 0)
    first, last = level == 0, level == half - 1

    def build(c):
        def rows(j, carry):
            r0 = pl.multiple_of(j * 64, 64)
            slot = lax.broadcasted_iota(jnp.int32, (64, BLOCK), 0) + r0
            cell = lax.broadcasted_iota(jnp.int32, (64, BLOCK), 1)
            here = slot == cell + HALO
            m0 = jnp.zeros((64, BLOCK), F32)
            m1 = jnp.zeros((64, BLOCK), F32)
            for k in range(NB):
                w0, w1 = MTV[0, pl.ds(k, 1), lanes(c)], MTV[1, pl.ds(k, 1), lanes(c)]
                hit = slot == NBV[pl.ds(k, 1), lanes(c)] - (y * slab + c * BLOCK)
                m0 = m0 + (jnp.where(hit, w0, 0.0) - jnp.where(here, w0, 0.0))
                m1 = m1 + (jnp.where(hit, w1, 0.0) - jnp.where(here, w1, 0.0))
            M[c, 0, pl.ds(r0, 64), :], M[c, 1, pl.ds(r0, 64), :] = split(m0)
            M[c, 2, pl.ds(r0, 64), :], M[c, 3, pl.ds(r0, 64), :] = split(m1)
            return carry

        lax.fori_loop(0, (BLOCK + 2 * HALO) // 64, rows, 0)

    def horizontal(s, c):
        window = pl.ds(pl.multiple_of(c * BLOCK, 128), BLOCK + 2 * HALO)
        uh, ul = split(X[s, 0, :, window])
        vh, vl = split(X[s, 1, :, window])
        ph, pl_ = split(X[s, 2, :, window])
        a0 = dot(jnp.concatenate([ph, uh, pl_, ul]), M[c, 0])
        b0 = dot(jnp.concatenate([ph, uh]), M[c, 1])
        a1 = dot(jnp.concatenate([ph, vh, pl_, vl]), M[c, 2])
        b1 = dot(jnp.concatenate([ph, vh]), M[c, 3])
        g0 = a0[: 2 * half] + a0[2 * half :] + b0
        g1 = a1[: 2 * half] + a1[2 * half :] + b1
        X[s + 1, 0, :, cells(c)] = X[s, 0, :, cells(c)] - g0[:half]
        X[s + 1, 1, :, cells(c)] = X[s, 1, :, cells(c)] - g1[:half]
        p = X[s, 2, :, cells(c)] - (g0[half:] + g1[half:])
        PP[s, :, lanes(c)] = p
        up = jnp.where(last, 0.0, pltpu.roll(p, half - 1, 0))
        down = jnp.where(first, 0.0, pltpu.roll(p, 1, 0))
        RS[s, :, lanes(c)] = X[s, 3, :, cells(c)] - C * (up - down)
        PB[s, c] = jnp.where(zh == 0, p[half - 1 :], p[:1])

    def vertical(s, c):
        top = jnp.where(zh == 0, 1.0, 0.0)
        own_b, other_b = PB[s, c], PQ[s, c]
        fix_own = jnp.where(last, -C * top, 0.0) + jnp.where(first, C * (1.0 - top), 0.0)
        fix_other = jnp.where(first, C * top, 0.0) + jnp.where(last, -C * (1.0 - top), 0.0)
        own = RS[s, :, lanes(c)] + fix_own * other_b
        other = RR[s, :, lanes(c)] + fix_other * own_b
        rh, rl = split(jnp.concatenate([own, other]))
        ih, il = IH[...], IL[...]
        w = dot(ih, rh) + (dot(ih, rl) + dot(il, rh))
        edge = jnp.where(zh == 0, w[half : half + 1], w[half + 7 : half + 8])
        w = w[:half]
        up = jnp.where(last, edge * top, pltpu.roll(w, half - 1, 0))
        down = jnp.where(first, edge * (1.0 - top), pltpu.roll(w, 1, 0))
        X[s + 1, 2, :, cells(c)] = PP[s, :, lanes(c)] - C * (up - down)
        X[s + 1, 3, :, cells(c)] = w

    def finish(t):
        s, c = t // blocks, order(t // blocks, t % blocks)
        for copy in z_copies(s, c):
            copy.wait()
        vertical(s, c)

        @pl.when((s < SUBSTEPS - 1) & (c == 0))
        def _():
            halo(s + 1, 0).start()

        @pl.when((s < SUBSTEPS - 1) & (c == blocks - 1))
        def _():
            halo(s + 1, 1).start()

        @pl.when(s == SUBSTEPS - 1)
        def _():
            for d in range(NY):
                y_out(1, c, d).start()
            y_out_wait(0, c)

            @pl.when(t % blocks >= TAIL)
            def _():
                y_out_wait(1, order(s, t % blocks - TAIL))

    def begin(t):
        s, i = t // blocks, t % blocks
        c = order(s, i)

        @pl.when(s == 0)
        def _():
            build(c)

            @pl.when(i == 0)
            def _():
                edge_wait(0)
                y_in_wait(0)

            y_in_wait(i)

            @pl.when(i == blocks - 1)
            def _():
                edge_wait(1)

            @pl.when(i + AHEAD < blocks)
            def _():
                y_in_start(i + AHEAD)

            @pl.when(i == 3)
            def _():
                edge_start(1)

        @pl.when(s == 1)
        def _():
            pl.when(i == 0)(lambda: y_in_sent(0))
            y_in_sent(i)

        @pl.when((s > 0) & (c == 0))
        def _():
            halo(s, 1).wait_recv()

        @pl.when((s > 0) & (c == blocks - 1))
        def _():
            halo(s, 0).wait_recv()

        horizontal(s, c)
        for copy in z_copies(s, c):
            copy.start()

        @pl.when(s == SUBSTEPS - 1)
        def _():
            for d in range(NY):
                y_out(0, c, d).start()

    def step(t, carry):
        @pl.when(t >= LAG)
        def _():
            finish(t - LAG)

        @pl.when(t < total)
        def _():
            begin(t)

        @pl.when(t == total)
        def _():
            for side in range(2):
                edge_drain(side)
                for s in range(1, SUBSTEPS):
                    halo(s, side).wait_send()

        return carry

    lax.fori_loop(0, total + LAG, step, 0)

    for i in range(blocks - TAIL, blocks):
        y_out_wait(1, order(SUBSTEPS - 1, i))


def per_device(prognostic, neighbours, metric, inverses):
    fields, rows16, cell_count = prognostic.shape
    half, slab = rows16 * NY, cell_count // NY
    blocks = slab // BLOCK
    dma = pltpu.SemaphoreType.DMA
    anywhere = pl.BlockSpec(memory_space=pltpu.HBM)
    return pl.pallas_call(
        kernel,
        name="acoustic",
        out_shape=jax.ShapeDtypeStruct(prognostic.shape, F32),
        in_specs=[anywhere, anywhere, anywhere, anywhere],
        out_specs=anywhere,
        scratch_shapes=[
            pltpu.VMEM((SUBSTEPS + 1, fields, half, slab + 2 * HALO), F32),
            pltpu.VMEM((SUBSTEPS, half, slab), F32),
            pltpu.VMEM((SUBSTEPS, half, slab), F32),
            pltpu.VMEM((SUBSTEPS, half, slab), F32),
            pltpu.VMEM((SUBSTEPS, blocks, 1, BLOCK), F32),
            pltpu.VMEM((SUBSTEPS, blocks, 1, BLOCK), F32),
            pltpu.VMEM((blocks, 4, BLOCK + 2 * HALO, BLOCK), BF16),
            pltpu.VMEM((2 * half, 2 * half), F32),
            pltpu.VMEM((NB, slab), jnp.int32),
            pltpu.VMEM((2, NB, slab), F32),
            pltpu.VMEM((half + 8, 2 * half), BF16),
            pltpu.VMEM((half + 8, 2 * half), BF16),
            dma((3,)),
            dma((2, blocks, NY - 1)),
            dma((2, blocks, NY - 1)),
            dma((2, blocks)),
            dma((2, blocks, NY - 1)),
            dma((2, blocks, NY - 1)),
            dma((2, blocks)),
            dma((SUBSTEPS, blocks)),
            dma((SUBSTEPS, blocks)),
            dma((SUBSTEPS, blocks)),
            dma((SUBSTEPS, blocks)),
            dma((SUBSTEPS, 2)),
            dma((SUBSTEPS, 2)),
            dma((2, NY)),
            dma((2, NY)),
            dma((2,)),
        ],
        compiler_params=pltpu.CompilerParams(
            collective_id=0, has_side_effects=True, vmem_limit_bytes=62 << 20
        ),
    )(prognostic, neighbours, metric, inverses)


def solution(mesh):
    in_specs = (
        P(None, "lev", "tile"),
        P(None, "tile"),
        P(None, None, "tile"),
        P("tile", None, None),
    )
    return jax.shard_map(
        per_device, mesh=mesh, in_specs=in_specs, out_specs=P(None, "lev", "tile"), check_vma=False
    )
```
